256 devices in a mesh: dp: 16 (over y, z_lo, core), own: 16 (over x, z_hi).
Axes of the slice: x: 4, y: 4, z: 8 (z_hi: 4, z_lo: 2; z = z_hi * 2 + z_lo), core: 2. Of those that a mesh axis runs over, the one named last changes fastest.
Arguments:
- grads: bfloat16 [16, 32, 768, 768], P('dp', 'own'), may hold values from -0.059814453 to 0.059814453
- owner: int32 [32], replicated, may hold values from 0 to 15, as said below
- weights: float32 [64, 768, 768], P('own', 'dp'), may hold values from -6 to 6
- stat_left: float32 [64, 768, 768], P('own', 'dp'), may hold values from -3 to 3
- stat_right: float32 [64, 768, 768], P('own', 'dp'), may hold values from -3 to 3
- adam_second: float32 [64, 768, 768], P('own', 'dp'), may hold values from 0.0002 to 1
- root_left: bfloat16 [64, 768, 768], P('own', 'dp'), may hold values from -0.21875 to 0.21875
- root_right: bfloat16 [64, 768, 768], P('own', 'dp'), may hold values from -0.21875 to 0.21875
Outputs:
- new_weights: bfloat16 [64, 768, 768], P('own')
- new_left: float32 [64, 768, 768], P('own', 'dp')
- new_right: float32 [64, 768, 768], P('own', 'dp')
- new_second: float32 [64, 768, 768], P('own', 'dp')
The draws below stay inside these ranges and needn't reach their ends.
Inputs may be any that keep to these rules, and one draw needn't show every extreme that they name: The 2 blocks 2 * j to 2 * j + 1 have different owners, for every j; one owner holds exactly 4 blocks and none holds more.
All inputs are finite; a program needn't handle non-finite values.
Results may differ from the reference program's by a relative error of at most 0.0095.
Values may be sent and summed in bfloat16 or wider, within the bound.
No kernel may reach another device: no remote copies, remote signals or barrier semaphores. Data moves between devices by JAX's collectives and lax.ppermute only.
A program may use at most 64 MiB of HBM per device.

```python
import math
import jax
import jax.numpy as jnp
from jax import lax

D = 768
BLOCK = 768
BPD = 2
NB = 32
CAP = 4
SLOTS = 64
N_DP = 16
N_OWN = 16


def draw_owner(key, part):
    key_start = jax.random.fold_in(key, 11)
    key_hot = jax.random.fold_in(key, 12)
    key_rows = jax.random.fold_in(key, 13)
    key_cols = jax.random.fold_in(key, 14)
    key_order = jax.random.fold_in(key, 15)
    start = jax.random.permutation(key_start, N_OWN).astype(jnp.int32)
    base = (start[:, None] + jnp.arange(BPD, dtype=jnp.int32)[None, :]) % N_OWN
    hot = jax.random.randint(key_hot, (), 0, N_OWN).astype(jnp.int32)
    present = jnp.any(base == hot, axis=1)
    score = jax.random.randint(key_rows, (N_OWN,), 0, 1 << 20).astype(jnp.int32) * N_OWN + jax.random.permutation(key_order, N_OWN).astype(jnp.int32)
    score = jnp.where(present, -1, score)
    picked_values, picked = lax.top_k(score, BPD)
    chosen = jnp.zeros((N_OWN,), jnp.int32).at[picked].set(1) > 0
    column = jax.random.randint(key_cols, (N_OWN,), 0, BPD).astype(jnp.int32)
    replace = chosen[:, None] & (jnp.arange(BPD, dtype=jnp.int32)[None, :] == column[:, None])
    result = jnp.where(replace, hot, base)
    return result.reshape(-1).astype(jnp.int32)


def draw_adam_second(key, part):
    key_slot = jax.random.fold_in(key, 21)
    key_col = jax.random.fold_in(key, 22)
    key_noise = jax.random.fold_in(key, 23)
    slot_factor = jnp.exp(jax.random.uniform(key_slot, (SLOTS, 1, 1), jnp.float32, math.log(0.3), math.log(3.0)))
    row_factor = (10.0 ** (jnp.arange(BLOCK, dtype=jnp.float32) / (BLOCK - 1)))[None, :, None]
    col_factor = jnp.exp(jax.random.uniform(key_col, (1, 1, D), jnp.float32, 0.0, math.log(3.0)))
    noise = jax.random.uniform(key_noise, (SLOTS, BLOCK, D), jnp.float32, 0.5, 2.0)
    return (0.0016 * slot_factor * row_factor * col_factor * noise).astype(jnp.float32)


def spiked(values, key, source, target, blocks, factor):
    def block_of(position):
        return (jnp.arange(values.shape[position]) // (values.shape[position] // blocks)).reshape((-1,) + (1,) * (values.ndim - 1 - position))

    first = jax.random.permutation(key, blocks)[block_of(target)]
    second = (block_of(target) + blocks // 2) % blocks
    return jnp.where((block_of(source) == first) | (block_of(source) == second), factor * values, values)


def steps_of(stream_key, extent, shards, low, top_value):
    def one(axis_at, blocks):
        heights = jax.random.uniform(jax.random.fold_in(jax.random.fold_in(stream_key, 6), axis_at), (blocks,), jnp.float32, low / len(shards), top_value / len(shards))
        return jnp.repeat(jnp.exp(heights), extent[axis_at] // blocks).reshape((-1,) + (1,) * (len(extent) - axis_at - 1))

    factor_of = one(*shards[0])
    for cut in shards[1:]:
        factor_of = factor_of * one(*cut)
    return factor_of


def gaussian(stream_key, shape, scale, bound, cuts=(), held_as=jnp.bfloat16):
    drawn = scale * jax.random.normal(stream_key, shape, jnp.float32)
    if cuts:
        drawn = drawn * steps_of(stream_key, shape, cuts, -0.22, 0.18)
    return jnp.clip(drawn, -bound, bound).astype(held_as)


def gaussian_with(rng, extent, scale, limit, shards, heavy, held_as=jnp.bfloat16):
    drawn = scale * jax.random.normal(rng, extent, jnp.float32)
    if shards:
        drawn = drawn * steps_of(rng, extent, shards, -0.22, 0.18)
    return jnp.clip(spiked(drawn, jax.random.fold_in(rng, 3), *heavy), -limit, limit).astype(held_as)


def setup_inputs(seed: int = 0) -> dict:
    arg_keys = jax.random.split(jax.random.key(seed), 9)
    grads = gaussian_with(arg_keys[0], (N_DP, NB, BLOCK, D), 0.01, 0.059814453, ((0, 16), (1, 16)), (0, 2, 16, 2.0))
    owner = draw_owner(jax.random.fold_in(arg_keys[8], 71), 0)
    weights = gaussian(arg_keys[2], (SLOTS, BLOCK, D), 1.0, 6.0, ((0, 16), (1, 16)), jnp.float32)
    stat_left = gaussian(arg_keys[3], (SLOTS, BLOCK, BLOCK), 0.5, 3.0, ((0, 16), (1, 16)), jnp.float32)
    stat_right = gaussian(arg_keys[4], (SLOTS, D, D), 0.5, 3.0, ((0, 16), (1, 16)), jnp.float32)
    adam_second = draw_adam_second(jax.random.fold_in(arg_keys[8], 71), 0)
    root_left = gaussian(arg_keys[6], (SLOTS, BLOCK, BLOCK), BLOCK ** -0.5, 0.21875, ((0, 16), (1, 16)))
    root_right = gaussian(arg_keys[7], (SLOTS, D, D), D ** -0.5, 0.21875, ((0, 16), (1, 16)))
    return dict(grads=grads, owner=owner, weights=weights, stat_left=stat_left, stat_right=stat_right, adam_second=adam_second, root_left=root_left, root_right=root_right)


def slot_index(owner):
    count = owner.shape[0]
    same = owner[:, None] == owner[None, :]
    earlier = jnp.arange(count, dtype=jnp.int32)[None, :] < jnp.arange(count, dtype=jnp.int32)[:, None]
    rank = lax.optimization_barrier(jnp.sum((same & earlier).astype(jnp.int32), axis=1)).astype(jnp.int32)
    return (owner * CAP + rank).astype(jnp.int32)

def reference(grads, owner, weights, stat_left, stat_right, adam_second, root_left, root_right):
    total = lax.optimization_barrier(jnp.sum(grads.astype(jnp.float32), axis=0)).astype(jnp.bfloat16)
    slot = slot_index(owner)
    slot_grad = jnp.zeros((SLOTS, BLOCK, D), jnp.bfloat16).at[slot].set(total)
    grad32 = slot_grad.astype(jnp.float32)
    new_left = 0.5 * stat_left + 0.5 * jnp.einsum('sij,skj->sik', grad32, grad32)
    new_right = 0.5 * stat_right + 0.5 * jnp.einsum('sji,sjk->sik', grad32, grad32)
    new_second = 0.9 * adam_second + 0.1 * grad32 * grad32
    adam_dir = grad32 / (jnp.sqrt(new_second) + 1e-08)
    half = jnp.einsum('sij,sjk->sik', root_left.astype(jnp.float32), grad32).astype(jnp.bfloat16)
    precond = jnp.einsum('sij,sjk->sik', half.astype(jnp.float32), root_right.astype(jnp.float32))
    adam_norm = jnp.sqrt(lax.optimization_barrier(jnp.sum(adam_dir * adam_dir, axis=(1, 2))))
    prec_norm = jnp.sqrt(lax.optimization_barrier(jnp.sum(precond * precond, axis=(1, 2))))
    graft = adam_norm / (prec_norm + 1e-06)
    new_weights = (weights - graft[:, None, None] * precond).astype(jnp.bfloat16)
    return (new_weights, new_left, new_right, new_second)
```

```python
import jax
import jax.numpy as jnp
from jax import lax
from jax.experimental import pallas as pl
from jax.experimental.pallas import tpu as pltpu
from jax.sharding import Mesh
from jax.sharding import PartitionSpec as P

Y, ZL, CORE, X, ZH = 4, 2, 2, 4, 4
CHIPS = Y * ZL
CAP = 4
BPD = 2
HALF = CAP // CORE
BF = jnp.bfloat16
F32 = jnp.float32


def slot_index(owner, capacity):
    count = owner.shape[0]
    same = owner[:, None] == owner[None, :]
    earlier = (
        jnp.arange(count, dtype=jnp.int32)[None, :] < jnp.arange(count, dtype=jnp.int32)[:, None]
    )
    rank = jnp.sum((same & earlier).astype(jnp.int32), axis=1)
    return owner * capacity + rank


def shift(axis, size, by):
    pairs = [(i, (i + by) % size) for i in range(size)]
    return lambda value: lax.ppermute(value, axis, pairs)


y_up, y_down = shift("y", Y, 1), shift("y", Y, Y - 1)
z_swap = shift("zl", ZL, 1)
core_swap = shift("core", CORE, 1)
zh_up, zh_down = shift("zh", ZH, 1), shift("zh", ZH, ZH - 1)


def gather_chips(mine):
    back, ahead, other = y_up(mine), y_down(mine), z_swap(mine)
    far0, far1 = y_up(back[0]), y_down(ahead[1])
    ob0, oa0 = y_up(other[0]), y_down(other[0])
    ob1, oa1 = z_swap(back[1]), z_swap(ahead[1])
    of0, of1 = y_up(ob0), z_swap(far1)
    return (mine, back, ahead, other, far0, far1, ob0, ob1, oa0, oa1, of0, of1)


def piece_rows(y, zl, rows):
    out = []
    for dy, dz in ((0, 0), (-1, 0), (1, 0), (0, 1), (2, 0), (-1, 1), (1, 1), (2, 1)):
        out.append((((y + dy) % Y) * ZL + (zl + dz) % ZL) * rows)
    return jnp.stack(out).astype(jnp.int32)


def piece_copies(refs, offs, dest, sems, base, rows, slot0=0):
    copies = ([], [])
    n = base
    for p in range(4):
        for s in range(2):
            copies[s].append(
                pltpu.make_async_copy(
                    refs[p].at[s],
                    dest.at[slot0 + s, pl.ds(pl.multiple_of(offs[p], 16), rows)],
                    sems.at[n],
                )
            )
            n += 1
    for p in range(4, 8):
        for s in range(2):
            copies[s].append(
                pltpu.make_async_copy(
                    refs[4 + 2 * (p - 4) + s],
                    dest.at[slot0 + s, pl.ds(pl.multiple_of(offs[p], 16), rows)],
                    sems.at[n],
                )
            )
            n += 1
    return copies


ANY = pl.BlockSpec(memory_space=pl.ANY)
VM = pl.BlockSpec(memory_space=pltpu.VMEM)
SM = pl.BlockSpec(memory_space=pltpu.SMEM)


def precond_body(offs, left, *refs):
    rows = left.shape[1]
    g_refs, r_refs = refs[:12], refs[12:24]
    prec, sums, g, r, sems = refs[24:]
    gc = piece_copies(g_refs, offs, g, sems, 0, rows)
    rc = piece_copies(r_refs, offs, r, sems, 16, rows)
    for s in range(2):
        for c in gc[s] + rc[s]:
            c.start()
    for s in range(2):
        for c in gc[s]:
            c.wait()
        half = jnp.dot(left[s], g[s], preferred_element_type=F32).astype(BF)
        for c in rc[s]:
            c.wait()
        out = jnp.dot(half, r[s], preferred_element_type=F32)
        prec[s] = out
        sums[s] = jnp.full((1, 128), jnp.sum(out * out), F32)


def precond_call(offs, left, g, r):
    slots, rows, width = left.shape
    return pl.pallas_call(
        precond_body,
        in_specs=[SM, VM] + [ANY] * 24,
        out_specs=[VM, VM],
        out_shape=[
            jax.ShapeDtypeStruct((slots, rows, width), F32),
            jax.ShapeDtypeStruct((slots, 1, 128), F32),
        ],
        scratch_shapes=[
            pltpu.VMEM((slots, width, width), BF),
            pltpu.VMEM((slots, width, width), BF),
            pltpu.SemaphoreType.DMA((32,)),
        ],
        compiler_params=pltpu.CompilerParams(vmem_limit_bytes=24 << 20),
        cost_estimate=pl.CostEstimate(
            flops=8 * rows * width * width, transcendentals=0, bytes_accessed=8 * width * width
        ),
        name="precond",
    )(offs, left, *g, *r)


def stats_body(offs, *refs):
    g_refs = refs[:12]
    lout, rout, g, sems = refs[12:]
    rows, width = lout.shape[1], lout.shape[2]
    gc = piece_copies(g_refs, offs, g, sems, 0, rows)
    for s in range(2):
        for c in gc[s]:
            c.start()
    first = offs[0]
    row_id = lax.broadcasted_iota(jnp.int32, (rows, width), 0) + first
    col_id = lax.broadcasted_iota(jnp.int32, (rows, width), 1)
    pick = (row_id == col_id).astype(BF)
    for s in range(2):
        for c in gc[s]:
            c.wait()
        full = g[s]
        own = g[s, pl.ds(pl.multiple_of(first, 16), rows)]
        nt = (((1,), (1,)), ((), ()))
        lout[s] = lax.dot_general(own, full, nt, preferred_element_type=F32)
        cols = lax.dot_general(pick, full, nt, preferred_element_type=F32).astype(BF)
        rout[s] = jnp.dot(cols, full, preferred_element_type=F32)


def stats_call(offs, g, rows):
    slots, _, width = g[0].shape
    return pl.pallas_call(
        stats_body,
        in_specs=[SM] + [ANY] * 12,
        out_specs=[VM, VM],
        out_shape=[jax.ShapeDtypeStruct((slots, rows, width), F32)] * 2,
        scratch_shapes=[
            pltpu.VMEM((slots, width, width), BF),
            pltpu.SemaphoreType.DMA((16,)),
        ],
        compiler_params=pltpu.CompilerParams(vmem_limit_bytes=24 << 20),
        cost_estimate=pl.CostEstimate(
            flops=12 * rows * width * width, transcendentals=0, bytes_accessed=4 * width * width
        ),
        name="stats",
    )(offs, *g)


def select_body(table, own, back, ahead, far0, far1, *refs):
    outs, (src, sems) = refs[:X], refs[X:]
    copies = []
    for n, ref in enumerate((own.at[0], own.at[1], back.at[0], back.at[1], ahead.at[0], ahead.at[1], far0, far1)):
        copies.append(pltpu.make_async_copy(ref, src.at[n], sems.at[n]))
    for c in copies:
        c.start()
    for c in copies:
        c.wait()
    for k in range(X):
        for s in range(CAP):
            at = table[k * CAP + s]

            @pl.when(at >= 0)
            def _(k=k, s=s, at=at):
                outs[k][s] = src[at]

            @pl.when(at < 0)
            def _(k=k, s=s):
                outs[k][s] = jnp.zeros(outs[k].shape[1:], BF)


def select_call(table, own, back, ahead, far0, far1):
    _, rows, width = own.shape
    return pl.pallas_call(
        select_body,
        in_specs=[SM] + [ANY] * 5,
        out_specs=[VM] * X,
        out_shape=[jax.ShapeDtypeStruct((CAP, rows, width), BF)] * X,
        scratch_shapes=[pltpu.VMEM((ZH * BPD, rows, width), BF), pltpu.SemaphoreType.DMA((8,))],
        compiler_params=pltpu.CompilerParams(vmem_limit_bytes=16 << 20),
        name="select",
    )(table, own, back, ahead, far0, far1)


def assemble_body(offs, *refs):
    mine, theirs = refs[:12], refs[12:24]
    out, sems = refs[24:]
    rows = mine[0].shape[1]
    at = offs[8]
    copies = []
    for pieces, base, start in ((mine, 0, at), (theirs, 16, HALF - at)):
        for group in piece_copies(pieces, offs, out, sems, base, rows, start):
            copies += group
    for c in copies:
        c.start()
    for c in copies:
        c.wait()


def assemble_call(offs, mine, theirs):
    slots, rows, width = mine[0].shape
    return pl.pallas_call(
        assemble_body,
        in_specs=[SM] + [ANY] * 24,
        out_specs=ANY,
        out_shape=jax.ShapeDtypeStruct((CORE * slots, CHIPS * rows, width), BF),
        scratch_shapes=[pltpu.SemaphoreType.DMA((32,))],
        name="assemble",
    )(offs, *mine, *theirs)


def on_device(grads, owner, weights, stat_left, stat_right, adam_second, root_left, root_right):
    y, zl, core, x, zh = (lax.axis_index(a) for a in ("y", "zl", "core", "x", "zh"))
    blocks, height, width = grads.shape[1:]
    rows = height // (CHIPS * CORE)

    def halves(value):
        return (
            lax.dynamic_slice_in_dim(value, HALF * core, HALF, 0),
            lax.dynamic_slice_in_dim(value, HALF * (1 - core), HALF, 0),
        )

    def join_rows(keep, came):
        return jnp.where(
            core == 0,
            jnp.concatenate([keep, came], axis=1),
            jnp.concatenate([came, keep], axis=1),
        )

    def to_chip_rows(value):
        keep, give = halves(value)
        return join_rows(keep, core_swap(give))

    def to_core_rows(value):
        keep = lax.dynamic_slice_in_dim(value, rows * core, rows, 1)
        give = lax.dynamic_slice_in_dim(value, rows * (1 - core), rows, 1)
        came = core_swap(give)
        return jnp.where(
            core == 0,
            jnp.concatenate([keep, came], axis=0),
            jnp.concatenate([came, keep], axis=0),
        )

    parts = grads[0].reshape(blocks, CHIPS, CORE, rows, width)
    keep = lax.dynamic_index_in_dim(parts, core, 2, False)
    give = lax.dynamic_index_in_dim(parts, 1 - core, 2, False)
    chip = (keep.astype(F32) + core_swap(give).astype(F32)).astype(BF)
    chip = jnp.swapaxes(chip, 0, 1)
    came = lax.all_to_all(chip, ("y", "zl"), 0, 0, tiled=True)
    summed = jnp.sum(came.astype(F32), axis=0).astype(BF)

    slot = slot_index(owner, CAP)
    index = jnp.stack(
        [
            (x * ZH + (zh + dz) % ZH) * BPD + i
            for dz, i in ((0, 0), (0, 1), (-1, 0), (-1, 1), (1, 0), (1, 1), (2, 0), (2, 1))
        ]
    )
    held = jnp.sum(
        jnp.where(index[:, None] == jnp.arange(slot.shape[0])[None, :], slot[None, :], 0), axis=1
    )
    k_id = jnp.arange(X * CAP, dtype=jnp.int32) // CAP
    s_id = jnp.arange(X * CAP, dtype=jnp.int32) % CAP
    target = (((x + k_id) % X) * ZH + zh) * CAP + s_id
    hit = held[None, :] == target[:, None]
    table = jnp.sum(jnp.where(hit, jnp.arange(1, 9, dtype=jnp.int32)[None, :], 0), axis=1) - 1

    right2 = to_chip_rows(root_right)
    left2 = to_chip_rows(root_left)
    weights2 = to_chip_rows(weights)
    right2, summed = lax.optimization_barrier((right2, summed))
    r_all = gather_chips(right2)
    back, ahead = zh_up(summed), zh_down(summed)
    far0, far1 = zh_up(back[0]), zh_down(ahead[1])
    sends = select_call(table, summed, back, ahead, far0, far1)
    mine = sends[0]
    for k in range(1, X):
        mine = mine + shift("x", X, k)(sends[k])

    g_own = to_chip_rows(mine)
    g_all = gather_chips(g_own)

    grad32 = mine.astype(F32)
    new_second = 0.9 * adam_second + 0.1 * grad32 * grad32
    adam_dir = grad32 / (jnp.sqrt(new_second) + 1e-08)
    adam_keep, adam_give = halves(jnp.sum(adam_dir * adam_dir, axis=(1, 2)))
    adam_sq = adam_keep + core_swap(adam_give)

    offs = jnp.concatenate([piece_rows(y, zl, CORE * rows), (HALF * core).astype(jnp.int32)[None]])
    precond, prec_sq = precond_call(offs, left2, g_all, r_all)
    part = jnp.concatenate([prec_sq[:, 0, :1], adam_sq[:, None]], axis=1)
    part = jnp.broadcast_to(part.reshape(1, 1, 4), (CHIPS, 1, 4))
    total = jnp.sum(lax.all_to_all(part, ("y", "zl"), 0, 0, tiled=True), axis=(0, 1)).reshape(HALF, 2)
    graft = jnp.sqrt(total[:, 1]) / (jnp.sqrt(total[:, 0]) + 1e-06)
    fresh = (weights2 - graft[:, None, None] * precond).astype(BF)

    n_all = gather_chips(fresh)
    n_other = tuple(core_swap(p) for p in n_all)
    new_weights = assemble_call(offs, n_all, n_other)

    lprod, rprod = stats_call(offs, g_all, CORE * rows)
    new_left = 0.5 * stat_left + 0.5 * to_core_rows(lprod)
    new_right = 0.5 * stat_right + 0.5 * to_core_rows(rprod)
    return (new_weights, new_left, new_right, new_second)


def solution(mesh):
    fine = Mesh(mesh.devices.reshape(Y, ZL, CORE, X, ZH), ("y", "zl", "core", "x", "zh"))
    dp, own = ("y", "zl", "core"), ("x", "zh")
    rows = P(own, dp, None)
    return jax.shard_map(
        on_device,
        mesh=fine,
        in_specs=(P(dp, own, None, None), P()) + (rows,) * 6,
        out_specs=(P(own, None, None), rows, rows, rows),
        check_vma=False,
    )
```

```python
import jax
import jax.numpy as jnp
from jax import lax
from jax.experimental import pallas as pl
from jax.experimental.pallas import tpu as pltpu
from jax.sharding import Mesh
from jax.sharding import PartitionSpec as P

Y, ZL, CORE, X, ZH = 4, 2, 2, 4, 4
CHIPS = Y * ZL
CAP = 4
BPD = 2
HALF = CAP // CORE
BF = jnp.bfloat16
F32 = jnp.float32


def slot_index(owner, capacity):
    count = owner.shape[0]
    same = owner[:, None] == owner[None, :]
    earlier = (
        jnp.arange(count, dtype=jnp.int32)[None, :] < jnp.arange(count, dtype=jnp.int32)[:, None]
    )
    rank = jnp.sum((same & earlier).astype(jnp.int32), axis=1)
    return owner * capacity + rank


def shift(axis, size, by):
    pairs = [(i, (i + by) % size) for i in range(size)]
    return lambda value: lax.ppermute(value, axis, pairs)


y_up, y_down = shift("y", Y, 1), shift("y", Y, Y - 1)
y_two = shift("y", Y, 2)
z_swap = shift("zl", ZL, 1)
core_swap = shift("core", CORE, 1)


def gather_chips(mine):
    back, ahead, other, far = y_up(mine), y_down(mine), z_swap(mine), y_two(mine)
    return (mine, back, ahead, other, far, y_up(other), y_down(other), z_swap(far))


def piece_rows(place_ref, rows):
    chip = place_ref[0] // CORE
    y, zl = chip // ZL, chip % ZL
    return [
        (((y + dy) % Y) * ZL + (zl + dz) % ZL) * rows
        for dy, dz in ((0, 0), (3, 0), (1, 0), (0, 1), (2, 0), (3, 1), (1, 1), (2, 1))
    ]


def place(refs, offs, dest, rows, slot0=0):
    for p in range(CHIPS):
        at = pl.ds(pl.multiple_of(offs[p], 16), rows)
        for s in range(HALF):
            dest[slot0 + s, at] = refs[p][s]


ANY = pl.BlockSpec(memory_space=pl.ANY)
HB = pl.BlockSpec(memory_space=pltpu.HBM)
VM = pl.BlockSpec(memory_space=pltpu.VMEM)
SM = pl.BlockSpec(memory_space=pltpu.SMEM)


def give_body(at_dp, grads, out, sems):
    copies = []
    for b in range(BPD):
        copies.append(pltpu.make_async_copy(grads.at[b, :, 1 - at_dp[0] % CORE], out.at[:, b], sems.at[b]))
    for c in copies:
        c.start()
    for c in copies:
        c.wait()


def give_call(at_dp, parts):
    blocks, chips, _, rows, width = parts.shape
    return pl.pallas_call(
        give_body,
        in_specs=[SM, ANY],
        out_specs=VM,
        out_shape=jax.ShapeDtypeStruct((chips, blocks, rows, width), BF),
        scratch_shapes=[pltpu.SemaphoreType.DMA((BPD,))],
        compiler_params=pltpu.CompilerParams(vmem_limit_bytes=4 << 20),
        name="give",
    )(at_dp, parts)


def pair_body(at_dp, grads, came, out, keep, sems):
    copies = []
    for b in range(BPD):
        copies.append(pltpu.make_async_copy(grads.at[b, :, at_dp[0] % CORE], keep.at[:, b], sems.at[b]))
    for c in copies:
        c.start()
    for c in copies:
        c.wait()
    for k in range(CHIPS):
        out[k] = (keep[k].astype(F32) + came[k].astype(F32)).astype(BF)


def pair_call(at_dp, parts, came):
    return pl.pallas_call(
        pair_body,
        in_specs=[SM, ANY, VM],
        out_specs=VM,
        out_shape=jax.ShapeDtypeStruct(came.shape, BF),
        scratch_shapes=[pltpu.VMEM(came.shape, BF), pltpu.SemaphoreType.DMA((BPD,))],
        compiler_params=pltpu.CompilerParams(vmem_limit_bytes=6 << 20),
        name="pair",
    )(at_dp, parts, came)


def precond_body(at_dp, adam_sq, left, *refs):
    rows = left.shape[1]
    g_refs, r_refs = refs[:CHIPS], refs[CHIPS : CHIPS + Y]
    prec, sums, g, r = refs[CHIPS + Y :]
    offs = piece_rows(at_dp, rows)
    place(g_refs, offs, g, rows)
    for p, n in enumerate((0, 1, 2, 4)):
        at = pl.ds(pl.multiple_of(offs[n] // (ZL * rows) * (ZL * rows), 16), ZL * rows)
        for s in range(HALF):
            r[s, at] = r_refs[p][s]
    lane = lax.broadcasted_iota(jnp.int32, (1, 128), 1)
    packed = jnp.zeros((1, 128), F32)
    for s in range(HALF):
        half = jnp.dot(left[s], g[s], preferred_element_type=F32).astype(BF)
        out = jnp.dot(half, r[s], preferred_element_type=F32)
        prec[s] = out
        packed = jnp.where(lane == s, jnp.sum(out * out), packed)
        packed = jnp.where(lane == HALF + s, adam_sq[s], packed)
    for k in range(CHIPS):
        sums[k] = packed


def precond_call(at_dp, adam_sq, left, g, r):
    slots, rows, width = left.shape
    return pl.pallas_call(
        precond_body,
        in_specs=[SM, SM] + [VM] * (1 + CHIPS + Y),
        out_specs=[VM] * 3,
        out_shape=[
            jax.ShapeDtypeStruct((slots, rows, width), F32),
            jax.ShapeDtypeStruct((CHIPS, 1, 128), F32),
            jax.ShapeDtypeStruct((slots, width, width), BF),
        ],
        scratch_shapes=[pltpu.VMEM((slots, width, width), BF)],
        compiler_params=pltpu.CompilerParams(vmem_limit_bytes=14 << 20),
        name="precond",
    )(at_dp, adam_sq, left, *g, *r)


def stats_body(at_dp, g, lout, rout):
    rows, width = lout.shape[1], lout.shape[2]
    first = piece_rows(at_dp, rows)[0]
    row_id = lax.broadcasted_iota(jnp.int32, (rows, width), 0) + first
    col_id = lax.broadcasted_iota(jnp.int32, (rows, width), 1)
    pick = (row_id == col_id).astype(BF)
    nt = (((1,), (1,)), ((), ()))
    for s in range(HALF):
        full = g[s]
        own = g[s, pl.ds(pl.multiple_of(first, 16), rows)]
        both = lax.dot_general(
            jnp.concatenate([own, pick], axis=0), full, nt, preferred_element_type=F32
        )
        lout[s] = both[:rows]
        rout[s] = jnp.dot(both[rows:].astype(BF), full, preferred_element_type=F32)


def stats_call(at_dp, g, rows):
    slots, _, width = g.shape
    return pl.pallas_call(
        stats_body,
        in_specs=[SM, VM],
        out_specs=[VM, VM],
        out_shape=[jax.ShapeDtypeStruct((slots, rows, width), F32)] * 2,
        compiler_params=pltpu.CompilerParams(vmem_limit_bytes=8 << 20),
        name="stats",
    )(at_dp, g)


def fresh_body(sums, weights, prec, out):
    total = sums[0]
    for k in range(1, CHIPS):
        total = total + sums[k]
    for s in range(HALF):
        prec_norm = jnp.sqrt(total[:, s : s + 1])
        adam_norm = jnp.sqrt(total[:, HALF + s : HALF + s + 1])
        graft = adam_norm / (prec_norm + 1e-06)
        out[s] = (weights[s] - graft * prec[s]).astype(BF)


def fresh_call(sums, weights, prec):
    return pl.pallas_call(
        fresh_body,
        in_specs=[VM] * 3,
        out_specs=VM,
        out_shape=jax.ShapeDtypeStruct(prec.shape, BF),
        compiler_params=pltpu.CompilerParams(vmem_limit_bytes=4 << 20),
        name="fresh",
    )(sums, weights, prec)


def sort_body(table, parts, out):
    for b in range(BPD):
        total = parts[0, b].astype(F32)
        for k in range(1, CHIPS):
            total = total + parts[k, b].astype(F32)
        total = total.astype(BF)
        for n in range(out.shape[0]):

            @pl.when(table[n] == b)
            def _(n=n, total=total):
                out[n] = total

    for n in range(out.shape[0]):

        @pl.when(table[n] < 0)
        def _(n=n):
            out[n] = jnp.zeros(out.shape[1:], BF)


def sort_call(table, parts):
    rows, width = parts.shape[2:]
    return pl.pallas_call(
        sort_body,
        in_specs=[SM, VM],
        out_specs=VM,
        out_shape=jax.ShapeDtypeStruct((table.shape[0], rows, width), BF),
        compiler_params=pltpu.CompilerParams(vmem_limit_bytes=5 << 20),
        name="sort",
    )(table, parts)


def pick_body(table, blocks, out):
    for n in range(out.shape[0]):
        at = table[n]
        block = blocks[jnp.maximum(at, 0)]
        out[n] = jnp.where(at >= 0, block, jnp.zeros_like(block))


def pick_call(table, blocks):
    _, rows, width = blocks.shape
    return pl.pallas_call(
        pick_body,
        in_specs=[SM, VM],
        out_specs=VM,
        out_shape=jax.ShapeDtypeStruct((table.shape[0], rows, width), BF),
        compiler_params=pltpu.CompilerParams(vmem_limit_bytes=4 << 20),
        name="pick",
    )(table, blocks)


def assemble_body(at_dp, *refs):
    mine, theirs, out = refs[:CHIPS], refs[CHIPS : 2 * CHIPS], refs[2 * CHIPS]
    rows = mine[0].shape[1]
    offs = piece_rows(at_dp, rows)
    at = HALF * (at_dp[0] % CORE)
    place(mine, offs, out, rows, at)
    place(theirs, offs, out, rows, HALF - at)


def assemble_call(at_dp, mine, theirs):
    slots, rows, width = mine[0].shape
    return pl.pallas_call(
        assemble_body,
        in_specs=[SM] + [VM] * (2 * CHIPS),
        out_specs=VM,
        out_shape=jax.ShapeDtypeStruct((CORE * slots, CHIPS * rows, width), BF),
        compiler_params=pltpu.CompilerParams(vmem_limit_bytes=12 << 20),
        name="assemble",
    )(at_dp, *mine, *theirs)


def on_device(grads, owner, weights, stat_left, stat_right, adam_second, root_left, root_right):
    y, zl, core, x, zh = (lax.axis_index(a) for a in ("y", "zl", "core", "x", "zh"))
    blocks, height, width = grads.shape[1:]
    rows = height // (CHIPS * CORE)

    def halves(value):
        return (
            lax.dynamic_slice_in_dim(value, HALF * core, HALF, 0),
            lax.dynamic_slice_in_dim(value, HALF * (1 - core), HALF, 0),
        )

    def join_rows(keep, came):
        return jnp.where(
            core == 0,
            jnp.concatenate([keep, came], axis=1),
            jnp.concatenate([came, keep], axis=1),
        )

    def to_chip_rows(value):
        keep, give = halves(value)
        return join_rows(keep, core_swap(give))

    def to_core_rows(value):
        keep = lax.dynamic_slice_in_dim(value, rows * core, rows, 1)
        give = lax.dynamic_slice_in_dim(value, rows * (1 - core), rows, 1)
        came = core_swap(give)
        return jnp.where(
            core == 0,
            jnp.concatenate([keep, came], axis=0),
            jnp.concatenate([came, keep], axis=0),
        )

    parts = grads[0].reshape(blocks, CHIPS, CORE, rows, width)
    at_dp = lax.axis_index(("y", "zl", "core")).astype(jnp.int32)[None]
    r_near = z_swap(root_right)
    chip = pair_call(at_dp, parts, core_swap(give_call(at_dp, parts)))
    chip, r_near = lax.optimization_barrier((chip, r_near))
    r_keep, r_give = halves(
        jnp.where(
            zl == 0, jnp.stack([root_right, r_near], axis=1), jnp.stack([r_near, root_right], axis=1)
        )
    )
    r_came = core_swap(r_give)
    pair = jnp.where(
        core == 0, jnp.stack([r_keep, r_came], axis=2), jnp.stack([r_came, r_keep], axis=2)
    ).reshape(HALF, ZL * CORE * rows, width)
    parts = lax.all_to_all(chip, ("y", "zl"), 0, 0, tiled=True)

    slot = slot_index(owner, CAP)
    owners = X * ZH
    me = x * ZH + zh
    mine_of = lax.dynamic_slice_in_dim(owner, me * BPD, BPD, 0)
    to = jnp.sum(
        jnp.where(
            mine_of[None, :] == jnp.arange(owners, dtype=jnp.int32)[:, None],
            jnp.arange(1, BPD + 1, dtype=jnp.int32)[None, :],
            0,
        ),
        axis=1,
    )
    to = to - 1
    target = me * CAP + jnp.arange(CAP, dtype=jnp.int32)
    source = jnp.arange(owners * BPD, dtype=jnp.int32) // BPD + 1
    held = jnp.sum(jnp.where(slot[None, :] == target[:, None], source[None, :], 0), axis=1) - 1

    left2 = to_chip_rows(root_left)
    weights2 = to_chip_rows(weights)
    left2, weights2, to, held, parts = lax.optimization_barrier(
        (left2, weights2, to, held, parts)
    )
    sends, pair = lax.optimization_barrier((sort_call(to, parts), pair))
    came = lax.all_to_all(sends, ("x", "zh"), 0, 0, tiled=True)
    r_all = (pair, y_up(pair), y_down(pair), y_two(pair))
    mine = pick_call(held, came)
    mine, r_all = lax.optimization_barrier((mine, r_all))

    g_own = to_chip_rows(mine)
    g_all = gather_chips(g_own)

    grad32 = mine.astype(F32)
    new_second = 0.9 * adam_second + 0.1 * grad32 * grad32
    adam_dir = grad32 / (jnp.sqrt(new_second) + 1e-08)
    adam_keep, adam_give = halves(jnp.sum(adam_dir * adam_dir, axis=(1, 2)))
    adam_sq = adam_keep + core_swap(adam_give)

    precond, sums, g_full = precond_call(at_dp, adam_sq, left2, g_all, r_all)
    sums = lax.all_to_all(sums, ("y", "zl"), 0, 0, tiled=True)
    lprod, rprod = stats_call(at_dp, g_full, CORE * rows)
    sums, lprod, rprod = lax.optimization_barrier((sums, lprod, rprod))
    fresh = fresh_call(sums, weights2, precond)
    new_left = 0.5 * stat_left + 0.5 * to_core_rows(lprod)
    new_right = 0.5 * stat_right + 0.5 * to_core_rows(rprod)

    n_all = gather_chips(fresh)
    n_other = tuple(core_swap(p) for p in n_all)
    new_weights = assemble_call(at_dp, n_all, n_other)
    return (new_weights, new_left, new_right, new_second)


def solution(mesh):
    fine = Mesh(mesh.devices.reshape(Y, ZL, CORE, X, ZH), ("y", "zl", "core", "x", "zh"))
    dp, own = ("y", "zl", "core"), ("x", "zh")
    rows = P(own, dp, None)
    return jax.shard_map(
        on_device,
        mesh=fine,
        in_specs=(P(dp, own, None, None), P()) + (rows,) * 6,
        out_specs=(P(own, None, None), rows, rows, rows),
        check_vma=False,
    )
```

```python
import jax
import jax.numpy as jnp
from jax import lax
from jax.experimental import pallas as pl
from jax.experimental.pallas import tpu as pltpu
from jax.sharding import Mesh
from jax.sharding import PartitionSpec as P

Y, ZL, CORE, X, ZH = 4, 2, 2, 4, 4
CHIPS = Y * ZL
CAP = 4
BPD = 2
HALF = CAP // CORE
BF = jnp.bfloat16
F32 = jnp.float32


def slot_index(owner, capacity):
    count = owner.shape[0]
    same = owner[:, None] == owner[None, :]
    earlier = (
        jnp.arange(count, dtype=jnp.int32)[None, :] < jnp.arange(count, dtype=jnp.int32)[:, None]
    )
    rank = jnp.sum((same & earlier).astype(jnp.int32), axis=1)
    return owner * capacity + rank


def shift(axis, size, by):
    pairs = [(i, (i + by) % size) for i in range(size)]
    return lambda value: lax.ppermute(value, axis, pairs)


y_up, y_down = shift("y", Y, 1), shift("y", Y, Y - 1)
y_two = shift("y", Y, 2)
z_swap = shift("zl", ZL, 1)
core_swap = shift("core", CORE, 1)


def gather_chips(mine, together):
    back, ahead, other, far = y_up(mine), y_down(mine), z_swap(mine), y_two(mine)
    if together:
        other, far = lax.optimization_barrier((other, far))
    return [mine, back, ahead, other, far, y_up(other), y_down(other), z_swap(far)]


def piece_rows(place_ref, rows):
    chip = place_ref[0] // CORE
    y, zl = chip // ZL, chip % ZL
    return [
        (((y + dy) % Y) * ZL + (zl + dz) % ZL) * rows
        for dy, dz in ((0, 0), (3, 0), (1, 0), (0, 1), (2, 0), (3, 1), (1, 1), (2, 1))
    ]


def place(refs, offs, dest, rows, slot0=0):
    for p in range(CHIPS):
        at = pl.ds(pl.multiple_of(offs[p], 16), rows)
        for s in range(HALF):
            dest[slot0 + s, at] = refs[p][s]


ANY = pl.BlockSpec(memory_space=pl.ANY)
HB = pl.BlockSpec(memory_space=pltpu.HBM)
VM = pl.BlockSpec(memory_space=pltpu.VMEM)
SM = pl.BlockSpec(memory_space=pltpu.SMEM)


def half_call(at_dp, parts, other):
    blocks, chips, _, rows, width = parts.shape

    def half_body(at_dp, grads, out, sems):
        core = at_dp[0] % CORE
        copies = []
        for b in range(BPD):
            src = grads.at[b, :, 1 - core if other else core]
            copies.append(pltpu.make_async_copy(src, out.at[:, b], sems.at[b]))
        for c in copies:
            c.start()
        for c in copies:
            c.wait()

    return pl.pallas_call(
        half_body,
        in_specs=[SM, ANY],
        out_specs=VM,
        out_shape=jax.ShapeDtypeStruct((chips, blocks, rows, width), BF),
        scratch_shapes=[pltpu.SemaphoreType.DMA((BPD,))],
        compiler_params=pltpu.CompilerParams(vmem_limit_bytes=4 << 20),
        name="give" if other else "keep",
    )(at_dp, parts)


def pair_body(keep, came, out):
    for k in range(CHIPS):
        out[k] = (keep[k].astype(F32) + came[k].astype(F32)).astype(BF)


def pair_call(keep, came):
    return pl.pallas_call(
        pair_body,
        in_specs=[VM, VM],
        out_specs=VM,
        out_shape=jax.ShapeDtypeStruct(came.shape, BF),
        compiler_params=pltpu.CompilerParams(vmem_limit_bytes=5 << 20),
        name="pair",
    )(keep, came)


def precond_body(at_dp, adam_sq, left, *refs):
    rows = left.shape[1]
    g_refs, r_refs = refs[:CHIPS], refs[CHIPS : CHIPS + Y]
    prec, sums, g, r, sems = refs[CHIPS + Y :]
    offs = piece_rows(at_dp, rows)
    copies = []
    for p, n in enumerate((0, 1, 2, 4)):
        at = pl.ds(pl.multiple_of(offs[n] // (ZL * rows) * (ZL * rows), 16), ZL * rows)
        copies.append(pltpu.make_async_copy(r_refs[p], r.at[:, at], sems.at[p]))
    for c in copies:
        c.start()
    place(g_refs, offs, g, rows)
    lane = lax.broadcasted_iota(jnp.int32, (1, 128), 1)
    packed = jnp.zeros((1, 128), F32)
    for s in range(HALF):
        half = jnp.dot(left[s], g[s], preferred_element_type=F32).astype(BF)
        if s == 0:
            for c in copies:
                c.wait()
        out = jnp.dot(half, r[s], preferred_element_type=F32)
        prec[s] = out
        packed = jnp.where(lane == s, jnp.sum(out * out), packed)
        packed = jnp.where(lane == HALF + s, adam_sq[s], packed)
    for k in range(CHIPS):
        sums[k] = packed


def precond_call(at_dp, adam_sq, left, g, r):
    slots, rows, width = left.shape
    r = [pltpu.with_memory_space_constraint(p, pltpu.HBM) for p in r]
    return pl.pallas_call(
        precond_body,
        in_specs=[SM, SM] + [VM] * (1 + CHIPS) + [ANY] * Y,
        out_specs=[VM] * 3,
        out_shape=[
            jax.ShapeDtypeStruct((slots, rows, width), F32),
            jax.ShapeDtypeStruct((CHIPS, 1, 128), F32),
            jax.ShapeDtypeStruct((slots, width, width), BF),
        ],
        scratch_shapes=[
            pltpu.VMEM((slots, width, width), BF),
            pltpu.SemaphoreType.DMA((Y,)),
        ],
        compiler_params=pltpu.CompilerParams(vmem_limit_bytes=6 << 20),
        name="precond",
    )(at_dp, adam_sq, left, *g, *r)


def stats_body(at_dp, g, lkeep, lgive, rkeep, rgive, prod):
    part, width = lkeep.shape[1], lkeep.shape[2]
    rows = CORE * part
    first = piece_rows(at_dp, rows)[0]
    row_id = lax.broadcasted_iota(jnp.int32, (rows, width), 0) + first
    col_id = lax.broadcasted_iota(jnp.int32, (rows, width), 1)
    pick = (row_id == col_id).astype(BF)
    nt = (((1,), (1,)), ((), ()))
    mine = pl.ds(pl.multiple_of(at_dp[0] % CORE * part, 16), part)
    theirs = pl.ds(pl.multiple_of((1 - at_dp[0] % CORE) * part, 16), part)
    for s in range(HALF):
        full = g[s]
        own = g[s, pl.ds(pl.multiple_of(first, 16), rows)]
        both = lax.dot_general(
            jnp.concatenate([own, pick], axis=0), full, nt, preferred_element_type=F32
        )
        prod[0, s] = both[:rows]
        prod[1, s] = jnp.dot(both[rows:].astype(BF), full, preferred_element_type=F32)
        for n, (keep, give) in enumerate(((lkeep, lgive), (rkeep, rgive))):
            keep[s] = prod[n, s, mine]
            give[s] = prod[n, s, theirs]


def stats_call(at_dp, g, rows):
    slots, _, width = g.shape
    return pl.pallas_call(
        stats_body,
        in_specs=[SM, VM],
        out_specs=[VM] * 4,
        out_shape=[jax.ShapeDtypeStruct((slots, rows, width), F32)] * 4,
        scratch_shapes=[pltpu.VMEM((2, slots, CORE * rows, width), F32)],
        compiler_params=pltpu.CompilerParams(vmem_limit_bytes=6 << 20),
        name="stats",
    )(at_dp, g)


def fresh_body(sums, weights, prec, out):
    total = sums[0]
    for k in range(1, CHIPS):
        total = total + sums[k]
    for s in range(HALF):
        prec_norm = jnp.sqrt(total[:, s : s + 1])
        adam_norm = jnp.sqrt(total[:, HALF + s : HALF + s + 1])
        graft = adam_norm / (prec_norm + 1e-06)
        out[s] = (weights[s] - graft * prec[s]).astype(BF)


def fresh_call(sums, weights, prec):
    return pl.pallas_call(
        fresh_body,
        in_specs=[VM] * 3,
        out_specs=VM,
        out_shape=jax.ShapeDtypeStruct(prec.shape, BF),
        compiler_params=pltpu.CompilerParams(vmem_limit_bytes=4 << 20),
        name="fresh",
    )(sums, weights, prec)


def sort_body(table, parts, out, totals):
    for b in range(BPD):
        total = parts[0, b].astype(F32)
        for k in range(1, CHIPS):
            total = total + parts[k, b].astype(F32)
        totals[b] = total.astype(BF)
    totals[BPD] = jnp.zeros(out.shape[1:], BF)
    for n in range(out.shape[0]):
        out[n] = totals[table[n]]


def sort_call(table, parts):
    rows, width = parts.shape[2:]
    return pl.pallas_call(
        sort_body,
        in_specs=[SM, VM],
        out_specs=VM,
        out_shape=jax.ShapeDtypeStruct((table.shape[0], rows, width), BF),
        scratch_shapes=[pltpu.VMEM((BPD + 1, rows, width), BF)],
        compiler_params=pltpu.CompilerParams(vmem_limit_bytes=5 << 20),
        name="sort",
    )(table, parts)


def pick_body(table, blocks, out):
    for n in range(out.shape[0]):
        at = table[n]
        block = blocks[jnp.maximum(at, 0)]
        out[n] = jnp.where(at >= 0, block, jnp.zeros_like(block))


def pick_call(table, blocks):
    _, rows, width = blocks.shape
    return pl.pallas_call(
        pick_body,
        in_specs=[SM, VM],
        out_specs=VM,
        out_shape=jax.ShapeDtypeStruct((table.shape[0], rows, width), BF),
        compiler_params=pltpu.CompilerParams(vmem_limit_bytes=4 << 20),
        name="pick",
    )(table, blocks)


def assemble_body(at_dp, *refs):
    pieces, out, sems = refs[: 2 * CHIPS], refs[2 * CHIPS], refs[2 * CHIPS + 1]
    rows = pieces[0].shape[1]
    offs = piece_rows(at_dp, rows)
    mine = HALF * (at_dp[0] % CORE)
    copies = []
    for n, piece in enumerate(pieces):
        first = mine if n < CHIPS else HALF - mine
        at = pl.ds(pl.multiple_of(offs[n % CHIPS], 16), rows)
        dest = out.at[pl.ds(first, HALF), at]
        copies.append(pltpu.make_async_copy(piece, dest, sems.at[n]))
    for c in copies:
        c.start()
    for c in copies:
        c.wait()


def assemble_call(at_dp, mine, theirs):
    slots, rows, width = mine[0].shape
    return pl.pallas_call(
        assemble_body,
        in_specs=[SM] + [VM] * (2 * CHIPS),
        out_specs=ANY,
        out_shape=jax.ShapeDtypeStruct((CORE * slots, CHIPS * rows, width), BF),
        scratch_shapes=[pltpu.SemaphoreType.DMA((2 * CHIPS,))],
        compiler_params=pltpu.CompilerParams(vmem_limit_bytes=7 << 20),
        name="assemble",
    )(at_dp, *mine, *theirs)


def on_device(grads, owner, weights, stat_left, stat_right, adam_second, root_left, root_right):
    y, zl, core, x, zh = (lax.axis_index(a) for a in ("y", "zl", "core", "x", "zh"))
    blocks, height, width = grads.shape[1:]
    rows = height // (CHIPS * CORE)

    def halves(value):
        return (
            lax.dynamic_slice_in_dim(value, HALF * core, HALF, 0),
            lax.dynamic_slice_in_dim(value, HALF * (1 - core), HALF, 0),
        )

    def join_rows(keep, came):
        return jnp.where(
            core == 0,
            jnp.concatenate([keep, came], axis=1),
            jnp.concatenate([came, keep], axis=1),
        )

    def to_chip_rows(value):
        keep, give = halves(value)
        return join_rows(keep, core_swap(give))

    def join_slots(keep, came):
        return jnp.where(
            core == 0,
            jnp.concatenate([keep, came], axis=0),
            jnp.concatenate([came, keep], axis=0),
        )

    parts = pltpu.with_memory_space_constraint(
        grads[0].reshape(blocks, CHIPS, CORE, rows, width), pltpu.HBM
    )
    at_dp = lax.axis_index(("y", "zl", "core")).astype(jnp.int32)[None]
    r_near = z_swap(root_right)
    chip = pair_call(half_call(at_dp, parts, False), core_swap(half_call(at_dp, parts, True)))
    chip, r_near = lax.optimization_barrier((chip, r_near))
    r_keep, r_give = halves(
        jnp.where(
            zl == 0, jnp.stack([root_right, r_near], axis=1), jnp.stack([r_near, root_right], axis=1)
        )
    )
    r_came = core_swap(r_give)
    pair = jnp.where(
        core == 0, jnp.stack([r_keep, r_came], axis=2), jnp.stack([r_came, r_keep], axis=2)
    ).reshape(HALF, ZL * CORE * rows, width)
    parts = lax.all_to_all(chip, ("y", "zl"), 0, 0, tiled=True)

    slot = slot_index(owner, CAP)
    owners = X * ZH
    me = x * ZH + zh
    mine_of = lax.dynamic_slice_in_dim(owner, me * BPD, BPD, 0)
    hit = mine_of[None, :] == jnp.arange(owners, dtype=jnp.int32)[:, None]
    order = jnp.arange(BPD, dtype=jnp.int32)
    to = BPD + jnp.maximum(jnp.sum(jnp.where(hit, order[None, :] - BPD, 0), axis=1), -BPD)
    target = me * CAP + jnp.arange(CAP, dtype=jnp.int32)
    source = jnp.arange(owners * BPD, dtype=jnp.int32) // BPD + 1
    held = jnp.sum(jnp.where(slot[None, :] == target[:, None], source[None, :], 0), axis=1) - 1

    left2 = to_chip_rows(root_left)
    weights2 = to_chip_rows(weights)
    left2, weights2, to, held, parts = lax.optimization_barrier(
        (left2, weights2, to, held, parts)
    )
    sends, pair = lax.optimization_barrier((sort_call(to, parts), pair))
    came = lax.all_to_all(sends, ("x", "zh"), 0, 0, tiled=True)
    r_all = (pair, y_up(pair), y_down(pair), y_two(pair))
    mine = pick_call(held, came)
    mine, r_all = lax.optimization_barrier((mine, r_all))

    g_all = gather_chips(to_chip_rows(mine), True)

    mine, _ = lax.optimization_barrier((mine, g_all[1]))
    grad32 = mine.astype(F32)
    new_second = 0.9 * adam_second + 0.1 * grad32 * grad32
    adam_dir = grad32 / (jnp.sqrt(new_second) + 1e-08)
    adam_keep, adam_give = halves(jnp.sum(adam_dir * adam_dir, axis=(1, 2)))
    adam_sq = adam_keep + core_swap(adam_give)

    precond, sums, g_full = precond_call(at_dp, adam_sq, left2, g_all, r_all)
    sums = lax.all_to_all(sums, ("y", "zl"), 0, 0, tiled=True)
    prods = stats_call(at_dp, g_full, rows)
    lkeep, lgive, rkeep, rgive = prods
    sums, lcame, rcame = lax.optimization_barrier((sums, core_swap(lgive), core_swap(rgive)))
    precond = pltpu.with_memory_space_constraint(precond, pltpu.HBM)
    fresh = fresh_call(sums, weights2, precond)

    n_all = gather_chips(fresh, False)
    n_all[:5] = lax.optimization_barrier(n_all[:5])
    new_left = 0.5 * stat_left + 0.5 * join_slots(lkeep, lcame)
    new_right = 0.5 * stat_right + 0.5 * join_slots(rkeep, rcame)
    n_all[7], new_left, new_right = lax.optimization_barrier((n_all[7], new_left, new_right))
    n_other = [core_swap(p) for p in n_all]
    new_weights = assemble_call(at_dp, n_all, n_other)
    return (new_weights, new_left, new_right, new_second)


def solution(mesh):
    fine = Mesh(mesh.devices.reshape(Y, ZL, CORE, X, ZH), ("y", "zl", "core", "x", "zh"))
    dp, own = ("y", "zl", "core"), ("x", "zh")
    rows = P(own, dp, None)
    return jax.shard_map(
        on_device,
        mesh=fine,
        in_specs=(P(dp, own, None, None), P()) + (rows,) * 6,
        out_specs=(P(own, None, None), rows, rows, rows),
        check_vma=False,
    )
```

```python
import jax
import jax.numpy as jnp
from jax import lax
from jax.experimental import pallas as pl
from jax.experimental.pallas import tpu as pltpu
from jax.sharding import Mesh
from jax.sharding import PartitionSpec as P

Y, ZL, CORE, X, ZH = 4, 2, 2, 4, 4
CHIPS = Y * ZL
CAP = 4
BPD = 2
HALF = CAP // CORE
BF = jnp.bfloat16
F32 = jnp.float32


def slot_index(owner, capacity):
    count = owner.shape[0]
    same = owner[:, None] == owner[None, :]
    earlier = (
        jnp.arange(count, dtype=jnp.int32)[None, :] < jnp.arange(count, dtype=jnp.int32)[:, None]
    )
    rank = jnp.sum((same & earlier).astype(jnp.int32), axis=1)
    return owner * capacity + rank


def shift(axis, size, by):
    pairs = [(i, (i + by) % size) for i in range(size)]
    return lambda value: lax.ppermute(value, axis, pairs)


y_up, y_down = shift("y", Y, 1), shift("y", Y, Y - 1)
y_two = shift("y", Y, 2)
z_swap = shift("zl", ZL, 1)
core_swap = shift("core", CORE, 1)


def gather_chips(mine):
    back, ahead, other, far = y_up(mine), y_down(mine), z_swap(mine), y_two(mine)
    other, far = lax.optimization_barrier((other, far))
    return [mine, back, ahead, other, far, y_up(other), y_down(other), z_swap(far)]


def piece_rows(place_ref, rows):
    chip = place_ref[0] // CORE
    y, zl = chip // ZL, chip % ZL
    return [
        (((y + dy) % Y) * ZL + (zl + dz) % ZL) * rows
        for dy, dz in ((0, 0), (3, 0), (1, 0), (0, 1), (2, 0), (3, 1), (1, 1), (2, 1))
    ]


def place(refs, offs, dest, rows, slot0=0):
    for p in range(CHIPS):
        at = pl.ds(pl.multiple_of(offs[p], 16), rows)
        for s in range(HALF):
            dest[slot0 + s, at] = refs[p][s]


ANY = pl.BlockSpec(memory_space=pl.ANY)
HB = pl.BlockSpec(memory_space=pltpu.HBM)
VM = pl.BlockSpec(memory_space=pltpu.VMEM)
SM = pl.BlockSpec(memory_space=pltpu.SMEM)


def half_call(at_dp, parts, other):
    blocks, chips, _, rows, width = parts.shape

    def half_body(at_dp, grads, out, sems):
        core = at_dp[0] % CORE
        copies = []
        for b in range(BPD):
            src = grads.at[b, :, 1 - core if other else core]
            copies.append(pltpu.make_async_copy(src, out.at[:, b], sems.at[b]))
        for c in copies:
            c.start()
        for c in copies:
            c.wait()

    return pl.pallas_call(
        half_body,
        in_specs=[SM, ANY],
        out_specs=VM,
        out_shape=jax.ShapeDtypeStruct((chips, blocks, rows, width), BF),
        scratch_shapes=[pltpu.SemaphoreType.DMA((BPD,))],
        compiler_params=pltpu.CompilerParams(vmem_limit_bytes=4 << 20),
        name="give" if other else "keep",
    )(at_dp, parts)


def pair_body(keep, came, out):
    for k in range(CHIPS):
        out[k] = (keep[k].astype(F32) + came[k].astype(F32)).astype(BF)


def pair_call(keep, came):
    return pl.pallas_call(
        pair_body,
        in_specs=[VM, VM],
        out_specs=VM,
        out_shape=jax.ShapeDtypeStruct(came.shape, BF),
        compiler_params=pltpu.CompilerParams(vmem_limit_bytes=5 << 20),
        name="pair",
    )(keep, came)


def precond_body(at_dp, adam_sq, left, *refs):
    rows = left.shape[1]
    g_refs, r_refs = refs[:CHIPS], refs[CHIPS : CHIPS + Y]
    prec, sums, g, r, sems = refs[CHIPS + Y :]
    offs = piece_rows(at_dp, rows)
    copies = []
    for p, n in enumerate((0, 1, 2, 4)):
        at = pl.ds(pl.multiple_of(offs[n] // (ZL * rows) * (ZL * rows), 16), ZL * rows)
        copies.append(pltpu.make_async_copy(r_refs[p], r.at[:, at], sems.at[p]))
    for c in copies:
        c.start()
    place(g_refs, offs, g, rows)
    lane = lax.broadcasted_iota(jnp.int32, (1, 128), 1)
    packed = jnp.zeros((1, 128), F32)
    for s in range(HALF):
        half = jnp.dot(left[s], g[s], preferred_element_type=F32).astype(BF)
        if s == 0:
            for c in copies:
                c.wait()
        out = jnp.dot(half, r[s], preferred_element_type=F32)
        prec[s] = out
        packed = jnp.where(lane == s, jnp.sum(out * out), packed)
        packed = jnp.where(lane == HALF + s, adam_sq[s], packed)
    for k in range(CHIPS):
        sums[k] = packed


def precond_call(at_dp, adam_sq, left, g, r):
    slots, rows, width = left.shape
    r = [pltpu.with_memory_space_constraint(p, pltpu.HBM) for p in r]
    return pl.pallas_call(
        precond_body,
        in_specs=[SM, SM] + [VM] * (1 + CHIPS) + [ANY] * Y,
        out_specs=[VM] * 3,
        out_shape=[
            jax.ShapeDtypeStruct((slots, rows, width), F32),
            jax.ShapeDtypeStruct((CHIPS, 1, 128), F32),
            jax.ShapeDtypeStruct((slots, width, width), BF),
        ],
        scratch_shapes=[
            pltpu.VMEM((slots, width, width), BF),
            pltpu.SemaphoreType.DMA((Y,)),
        ],
        compiler_params=pltpu.CompilerParams(vmem_limit_bytes=6 << 20),
        name="precond",
    )(at_dp, adam_sq, left, *g, *r)


def stats_body(at_dp, g, lkeep, lgive, rkeep, rgive, prod):
    part, width = lkeep.shape[1], lkeep.shape[2]
    rows = CORE * part
    first = piece_rows(at_dp, rows)[0]
    row_id = lax.broadcasted_iota(jnp.int32, (rows, width), 0) + first
    col_id = lax.broadcasted_iota(jnp.int32, (rows, width), 1)
    pick = (row_id == col_id).astype(BF)
    nt = (((1,), (1,)), ((), ()))
    mine = pl.ds(pl.multiple_of(at_dp[0] % CORE * part, 16), part)
    theirs = pl.ds(pl.multiple_of((1 - at_dp[0] % CORE) * part, 16), part)
    for s in range(HALF):
        full = g[s]
        own = g[s, pl.ds(pl.multiple_of(first, 16), rows)]
        both = lax.dot_general(
            jnp.concatenate([own, pick], axis=0), full, nt, preferred_element_type=F32
        )
        prod[0, s] = both[:rows]
        prod[1, s] = jnp.dot(both[rows:].astype(BF), full, preferred_element_type=F32)
        for n, (keep, give) in enumerate(((lkeep, lgive), (rkeep, rgive))):
            keep[s] = prod[n, s, mine]
            give[s] = prod[n, s, theirs]


def stats_call(at_dp, g, rows):
    slots, _, width = g.shape
    return pl.pallas_call(
        stats_body,
        in_specs=[SM, VM],
        out_specs=[VM] * 4,
        out_shape=[jax.ShapeDtypeStruct((slots, rows, width), F32)] * 4,
        scratch_shapes=[pltpu.VMEM((2, slots, CORE * rows, width), F32)],
        compiler_params=pltpu.CompilerParams(vmem_limit_bytes=6 << 20),
        name="stats",
    )(at_dp, g)


def fresh_body(sums, weights, prec, out):
    total = sums[0]
    for k in range(1, CHIPS):
        total = total + sums[k]
    for s in range(HALF):
        prec_norm = jnp.sqrt(total[:, s : s + 1])
        adam_norm = jnp.sqrt(total[:, HALF + s : HALF + s + 1])
        graft = adam_norm / (prec_norm + 1e-06)
        out[s] = (weights[s] - graft * prec[s]).astype(BF)


def fresh_call(sums, weights, prec):
    return pl.pallas_call(
        fresh_body,
        in_specs=[VM] * 3,
        out_specs=VM,
        out_shape=jax.ShapeDtypeStruct(prec.shape, BF),
        compiler_params=pltpu.CompilerParams(vmem_limit_bytes=4 << 20),
        name="fresh",
    )(sums, weights, prec)


def sort_body(table, parts, out, totals):
    for b in range(BPD):
        total = parts[0, b].astype(F32)
        for k in range(1, CHIPS):
            total = total + parts[k, b].astype(F32)
        totals[b] = total.astype(BF)
    totals[BPD] = jnp.zeros(out.shape[1:], BF)
    for n in range(out.shape[0]):
        out[n] = totals[table[n]]


def sort_call(table, parts):
    rows, width = parts.shape[2:]
    return pl.pallas_call(
        sort_body,
        in_specs=[SM, VM],
        out_specs=VM,
        out_shape=jax.ShapeDtypeStruct((table.shape[0], rows, width), BF),
        scratch_shapes=[pltpu.VMEM((BPD + 1, rows, width), BF)],
        compiler_params=pltpu.CompilerParams(vmem_limit_bytes=5 << 20),
        name="sort",
    )(table, parts)


def pick_body(table, blocks, out):
    for n in range(out.shape[0]):
        at = table[n]
        block = blocks[jnp.maximum(at, 0)]
        out[n] = jnp.where(at >= 0, block, jnp.zeros_like(block))


def pick_call(table, blocks):
    _, rows, width = blocks.shape
    return pl.pallas_call(
        pick_body,
        in_specs=[SM, VM],
        out_specs=VM,
        out_shape=jax.ShapeDtypeStruct((table.shape[0], rows, width), BF),
        compiler_params=pltpu.CompilerParams(vmem_limit_bytes=4 << 20),
        name="pick",
    )(table, blocks)


def assemble_body(at_dp, *refs):
    pieces, out, sems = refs[: 2 * CHIPS], refs[2 * CHIPS], refs[2 * CHIPS + 1]
    rows = pieces[0].shape[1]
    offs = piece_rows(at_dp, rows)
    mine = HALF * (at_dp[0] % CORE)
    copies = []
    for n, piece in enumerate(pieces):
        first = mine if n < CHIPS else HALF - mine
        at = pl.ds(pl.multiple_of(offs[n % CHIPS], 16), rows)
        dest = out.at[pl.ds(first, HALF), at]
        copies.append(pltpu.make_async_copy(piece, dest, sems.at[n]))
    for c in copies:
        c.start()
    for c in copies:
        c.wait()


def assemble_call(at_dp, mine, theirs):
    slots, rows, width = mine[0].shape
    return pl.pallas_call(
        assemble_body,
        in_specs=[SM] + [VM] * (2 * CHIPS),
        out_specs=ANY,
        out_shape=jax.ShapeDtypeStruct((CORE * slots, CHIPS * rows, width), BF),
        scratch_shapes=[pltpu.SemaphoreType.DMA((2 * CHIPS,))],
        compiler_params=pltpu.CompilerParams(vmem_limit_bytes=7 << 20),
        name="assemble",
    )(at_dp, *mine, *theirs)


def on_device(grads, owner, weights, stat_left, stat_right, adam_second, root_left, root_right):
    y, zl, core, x, zh = (lax.axis_index(a) for a in ("y", "zl", "core", "x", "zh"))
    blocks, height, width = grads.shape[1:]
    rows = height // (CHIPS * CORE)

    def halves(value):
        return (
            lax.dynamic_slice_in_dim(value, HALF * core, HALF, 0),
            lax.dynamic_slice_in_dim(value, HALF * (1 - core), HALF, 0),
        )

    def join_rows(keep, came):
        return jnp.where(
            core == 0,
            jnp.concatenate([keep, came], axis=1),
            jnp.concatenate([came, keep], axis=1),
        )

    def to_chip_rows(value):
        keep, give = halves(value)
        return join_rows(keep, core_swap(give))

    def join_slots(keep, came):
        return jnp.where(
            core == 0,
            jnp.concatenate([keep, came], axis=0),
            jnp.concatenate([came, keep], axis=0),
        )

    parts = pltpu.with_memory_space_constraint(
        grads[0].reshape(blocks, CHIPS, CORE, rows, width), pltpu.HBM
    )
    at_dp = lax.axis_index(("y", "zl", "core")).astype(jnp.int32)[None]
    r_near = z_swap(root_right)
    chip = pair_call(half_call(at_dp, parts, False), core_swap(half_call(at_dp, parts, True)))
    chip, r_near = lax.optimization_barrier((chip, r_near))
    r_keep, r_give = halves(
        jnp.where(
            zl == 0, jnp.stack([root_right, r_near], axis=1), jnp.stack([r_near, root_right], axis=1)
        )
    )
    r_came = core_swap(r_give)
    pair = jnp.where(
        core == 0, jnp.stack([r_keep, r_came], axis=2), jnp.stack([r_came, r_keep], axis=2)
    ).reshape(HALF, ZL * CORE * rows, width)
    parts = lax.all_to_all(chip, ("y", "zl"), 0, 0, tiled=True)

    slot = slot_index(owner, CAP)
    owners = X * ZH
    me = x * ZH + zh
    mine_of = lax.dynamic_slice_in_dim(owner, me * BPD, BPD, 0)
    hit = mine_of[None, :] == jnp.arange(owners, dtype=jnp.int32)[:, None]
    order = jnp.arange(BPD, dtype=jnp.int32)
    to = BPD + jnp.maximum(jnp.sum(jnp.where(hit, order[None, :] - BPD, 0), axis=1), -BPD)
    target = me * CAP + jnp.arange(CAP, dtype=jnp.int32)
    source = jnp.arange(owners * BPD, dtype=jnp.int32) // BPD + 1
    held = jnp.sum(jnp.where(slot[None, :] == target[:, None], source[None, :], 0), axis=1) - 1

    left2 = to_chip_rows(root_left)
    weights2 = to_chip_rows(weights)
    left2, weights2, to, held, parts = lax.optimization_barrier(
        (left2, weights2, to, held, parts)
    )
    sends, pair = lax.optimization_barrier((sort_call(to, parts), pair))
    came = lax.all_to_all(sends, ("x", "zh"), 0, 0, tiled=True)
    r_all = (pair, y_up(pair), y_down(pair), y_two(pair))
    mine = pick_call(held, came)
    mine, r_all = lax.optimization_barrier((mine, r_all))

    g_all = gather_chips(to_chip_rows(mine))

    mine, _ = lax.optimization_barrier((mine, g_all[1]))
    grad32 = mine.astype(F32)
    new_second = 0.9 * adam_second + 0.1 * grad32 * grad32
    adam_dir = grad32 / (jnp.sqrt(new_second) + 1e-08)
    adam_keep, adam_give = halves(jnp.sum(adam_dir * adam_dir, axis=(1, 2)))
    adam_sq = adam_keep + core_swap(adam_give)

    precond, sums, g_full = precond_call(at_dp, adam_sq, left2, g_all, r_all)
    sums = lax.all_to_all(sums, ("y", "zl"), 0, 0, tiled=True)
    prods = stats_call(at_dp, g_full, rows)
    lkeep, lgive, rkeep, rgive = prods
    sums, lcame, rcame = lax.optimization_barrier((sums, core_swap(lgive), core_swap(rgive)))
    precond = pltpu.with_memory_space_constraint(precond, pltpu.HBM)
    fresh = fresh_call(sums, weights2, precond)

    n_all = gather_chips(fresh)
    n_all[:5] = lax.optimization_barrier(n_all[:5])
    new_left = 0.5 * stat_left + 0.5 * join_slots(lkeep, lcame)
    new_right = 0.5 * stat_right + 0.5 * join_slots(rkeep, rcame)
    n_all[7], new_left, new_right = lax.optimization_barrier((n_all[7], new_left, new_right))
    n_other = [core_swap(p) for p in n_all]
    new_weights = assemble_call(at_dp, n_all, n_other)
    return (new_weights, new_left, new_right, new_second)


def solution(mesh):
    fine = Mesh(mesh.devices.reshape(Y, ZL, CORE, X, ZH), ("y", "zl", "core", "x", "zh"))
    dp, own = ("y", "zl", "core"), ("x", "zh")
    rows = P(own, dp, None)
    return jax.shard_map(
        on_device,
        mesh=fine,
        in_specs=(P(dp, own, None, None), P()) + (rows,) * 6,
        out_specs=(P(own, None, None), rows, rows, rows),
        check_vma=False,
    )
```

```python
import jax
import jax.numpy as jnp
from jax import lax
from jax.experimental import pallas as pl
from jax.experimental.pallas import tpu as pltpu
from jax.sharding import Mesh
from jax.sharding import PartitionSpec as P

Y, ZL, CORE, X, ZH = 4, 2, 2, 4, 4
CHIPS = Y * ZL
CAP = 4
BPD = 2
HALF = CAP // CORE
BF = jnp.bfloat16
F32 = jnp.float32


def slot_index(owner, capacity):
    count = owner.shape[0]
    same = owner[:, None] == owner[None, :]
    earlier = (
        jnp.arange(count, dtype=jnp.int32)[None, :] < jnp.arange(count, dtype=jnp.int32)[:, None]
    )
    rank = jnp.sum((same & earlier).astype(jnp.int32), axis=1)
    return owner * capacity + rank


def shift(axis, size, by):
    pairs = [(i, (i + by) % size) for i in range(size)]
    return lambda value: lax.ppermute(value, axis, pairs)


y_up, y_down = shift("y", Y, 1), shift("y", Y, Y - 1)
y_two = shift("y", Y, 2)
z_swap = shift("zl", ZL, 1)
core_swap = shift("core", CORE, 1)


def gather_chips(mine):
    back, ahead, other, far = y_up(mine), y_down(mine), z_swap(mine), y_two(mine)
    other, far = lax.optimization_barrier((other, far))
    return [mine, back, ahead, other, far, y_up(other), y_down(other), z_swap(far)]


def piece_rows(place_ref, rows):
    chip = place_ref[0] // CORE
    y, zl = chip // ZL, chip % ZL
    return [
        (((y + dy) % Y) * ZL + (zl + dz) % ZL) * rows
        for dy, dz in ((0, 0), (3, 0), (1, 0), (0, 1), (2, 0), (3, 1), (1, 1), (2, 1))
    ]


def place(refs, offs, dest, rows, slot0=0):
    for p in range(CHIPS):
        at = pl.ds(pl.multiple_of(offs[p], 16), rows)
        for s in range(HALF):
            dest[slot0 + s, at] = refs[p][s]


ANY = pl.BlockSpec(memory_space=pl.ANY)
HB = pl.BlockSpec(memory_space=pltpu.HBM)
VM = pl.BlockSpec(memory_space=pltpu.VMEM)
SM = pl.BlockSpec(memory_space=pltpu.SMEM)


def half_call(at_dp, parts, other):
    blocks, chips, _, rows, width = parts.shape

    def half_body(at_dp, grads, out, sems):
        core = at_dp[0] % CORE
        copies = []
        for b in range(BPD):
            src = grads.at[b, :, 1 - core if other else core]
            copies.append(pltpu.make_async_copy(src, out.at[:, b], sems.at[b]))
        for c in copies:
            c.start()
        for c in copies:
            c.wait()

    return pl.pallas_call(
        half_body,
        in_specs=[SM, ANY],
        out_specs=VM,
        out_shape=jax.ShapeDtypeStruct((chips, blocks, rows, width), BF),
        scratch_shapes=[pltpu.SemaphoreType.DMA((BPD,))],
        compiler_params=pltpu.CompilerParams(vmem_limit_bytes=4 << 20),
        name="give" if other else "keep",
    )(at_dp, parts)


def pair_body(keep, came, out):
    for k in range(CHIPS):
        out[k] = (keep[k].astype(F32) + came[k].astype(F32)).astype(BF)


def pair_call(keep, came):
    return pl.pallas_call(
        pair_body,
        in_specs=[VM, VM],
        out_specs=VM,
        out_shape=jax.ShapeDtypeStruct(came.shape, BF),
        compiler_params=pltpu.CompilerParams(vmem_limit_bytes=5 << 20),
        name="pair",
    )(keep, came)


def precond_body(at_dp, adam_sq, left, *refs):
    rows = left.shape[1]
    g_refs, r_refs = refs[:CHIPS], refs[CHIPS : CHIPS + Y]
    prec, sums, g, r, sems = refs[CHIPS + Y :]
    offs = piece_rows(at_dp, rows)
    copies = []
    for p, n in enumerate((0, 1, 2, 4)):
        at = pl.ds(pl.multiple_of(offs[n] // (ZL * rows) * (ZL * rows), 16), ZL * rows)
        copies.append(pltpu.make_async_copy(r_refs[p], r.at[:, at], sems.at[p]))
    for c in copies:
        c.start()
    place(g_refs, offs, g, rows)
    lane = lax.broadcasted_iota(jnp.int32, (1, 128), 1)
    packed = jnp.zeros((1, 128), F32)
    for s in range(HALF):
        half = jnp.dot(left[s], g[s], preferred_element_type=F32).astype(BF)
        if s == 0:
            for c in copies:
                c.wait()
        out = jnp.dot(half, r[s], preferred_element_type=F32)
        prec[s] = out
        packed = jnp.where(lane == s, jnp.sum(out * out), packed)
        packed = jnp.where(lane == HALF + s, adam_sq[s], packed)
    for k in range(CHIPS):
        sums[k] = packed


def precond_call(at_dp, adam_sq, left, g, r):
    slots, rows, width = left.shape
    r = [pltpu.with_memory_space_constraint(p, pltpu.HBM) for p in r]
    return pl.pallas_call(
        precond_body,
        in_specs=[SM, SM] + [VM] * (1 + CHIPS) + [ANY] * Y,
        out_specs=[VM] * 3,
        out_shape=[
            jax.ShapeDtypeStruct((slots, rows, width), F32),
            jax.ShapeDtypeStruct((CHIPS, 1, 128), F32),
            jax.ShapeDtypeStruct((slots, width, width), BF),
        ],
        scratch_shapes=[
            pltpu.VMEM((slots, width, width), BF),
            pltpu.SemaphoreType.DMA((Y,)),
        ],
        compiler_params=pltpu.CompilerParams(vmem_limit_bytes=6 << 20),
        name="precond",
    )(at_dp, adam_sq, left, *g, *r)


def stats_body(at_dp, g, lkeep, lgive, rkeep, rgive, prod):
    part, width = lkeep.shape[1], lkeep.shape[2]
    rows = CORE * part
    first = piece_rows(at_dp, rows)[0]
    row_id = lax.broadcasted_iota(jnp.int32, (rows, width), 0) + first
    col_id = lax.broadcasted_iota(jnp.int32, (rows, width), 1)
    pick = (row_id == col_id).astype(BF)
    nt = (((1,), (1,)), ((), ()))
    mine = pl.ds(pl.multiple_of(at_dp[0] % CORE * part, 16), part)
    theirs = pl.ds(pl.multiple_of((1 - at_dp[0] % CORE) * part, 16), part)
    for s in range(HALF):
        full = g[s]
        own = g[s, pl.ds(pl.multiple_of(first, 16), rows)]
        both = lax.dot_general(
            jnp.concatenate([own, pick], axis=0), full, nt, preferred_element_type=F32
        )
        prod[0, s] = both[:rows]
        prod[1, s] = jnp.dot(both[rows:].astype(BF), full, preferred_element_type=F32)
        for n, (keep, give) in enumerate(((lkeep, lgive), (rkeep, rgive))):
            keep[s] = prod[n, s, mine]
            give[s] = prod[n, s, theirs]


def stats_call(at_dp, g, rows):
    slots, _, width = g.shape
    return pl.pallas_call(
        stats_body,
        in_specs=[SM, VM],
        out_specs=[VM] * 4,
        out_shape=[jax.ShapeDtypeStruct((slots, rows, width), F32)] * 4,
        scratch_shapes=[pltpu.VMEM((2, slots, CORE * rows, width), F32)],
        compiler_params=pltpu.CompilerParams(vmem_limit_bytes=6 << 20),
        name="stats",
    )(at_dp, g)


def fresh_body(sums, weights, prec, out):
    total = sums[0]
    for k in range(1, CHIPS):
        total = total + sums[k]
    for s in range(HALF):
        prec_norm = jnp.sqrt(total[:, s : s + 1])
        adam_norm = jnp.sqrt(total[:, HALF + s : HALF + s + 1])
        graft = adam_norm / (prec_norm + 1e-06)
        out[s] = (weights[s] - graft * prec[s]).astype(BF)


def fresh_call(sums, weights, prec):
    return pl.pallas_call(
        fresh_body,
        in_specs=[VM] * 3,
        out_specs=VM,
        out_shape=jax.ShapeDtypeStruct(prec.shape, BF),
        compiler_params=pltpu.CompilerParams(vmem_limit_bytes=4 << 20),
        name="fresh",
    )(sums, weights, prec)


def sort_body(table, parts, out, totals):
    for b in range(BPD):
        total = parts[0, b].astype(F32)
        for k in range(1, CHIPS):
            total = total + parts[k, b].astype(F32)
        totals[b] = total.astype(BF)
    totals[BPD] = jnp.zeros(out.shape[1:], BF)
    for n in range(out.shape[0]):
        out[n] = totals[table[n]]


def sort_call(table, parts):
    rows, width = parts.shape[2:]
    return pl.pallas_call(
        sort_body,
        in_specs=[SM, VM],
        out_specs=VM,
        out_shape=jax.ShapeDtypeStruct((table.shape[0], rows, width), BF),
        scratch_shapes=[pltpu.VMEM((BPD + 1, rows, width), BF)],
        compiler_params=pltpu.CompilerParams(vmem_limit_bytes=5 << 20),
        name="sort",
    )(table, parts)


def pick_body(table, blocks, out):
    for n in range(out.shape[0]):
        at = table[n]
        block = blocks[jnp.maximum(at, 0)]
        out[n] = jnp.where(at >= 0, block, jnp.zeros_like(block))


def pick_call(table, blocks):
    _, rows, width = blocks.shape
    return pl.pallas_call(
        pick_body,
        in_specs=[SM, VM],
        out_specs=VM,
        out_shape=jax.ShapeDtypeStruct((table.shape[0], rows, width), BF),
        compiler_params=pltpu.CompilerParams(vmem_limit_bytes=4 << 20),
        name="pick",
    )(table, blocks)


def assemble_body(at_dp, *refs):
    pieces, out, sems = refs[: 2 * CHIPS], refs[2 * CHIPS], refs[2 * CHIPS + 1]
    rows = pieces[0].shape[1]
    offs = piece_rows(at_dp, rows)
    mine = HALF * (at_dp[0] % CORE)
    copies = []
    for n, piece in enumerate(pieces):
        first = mine if n < CHIPS else HALF - mine
        at = pl.ds(pl.multiple_of(offs[n % CHIPS], 16), rows)
        dest = out.at[pl.ds(first, HALF), at]
        copies.append(pltpu.make_async_copy(piece, dest, sems.at[n]))
    for c in copies:
        c.start()
    for c in copies:
        c.wait()


def assemble_call(at_dp, mine, theirs):
    slots, rows, width = mine[0].shape
    return pl.pallas_call(
        assemble_body,
        in_specs=[SM] + [VM] * (2 * CHIPS),
        out_specs=ANY,
        out_shape=jax.ShapeDtypeStruct((CORE * slots, CHIPS * rows, width), BF),
        scratch_shapes=[pltpu.SemaphoreType.DMA((2 * CHIPS,))],
        compiler_params=pltpu.CompilerParams(vmem_limit_bytes=7 << 20),
        name="assemble",
    )(at_dp, *mine, *theirs)


def on_device(grads, owner, weights, stat_left, stat_right, adam_second, root_left, root_right):
    y, zl, core, x, zh = (lax.axis_index(a) for a in ("y", "zl", "core", "x", "zh"))
    blocks, height, width = grads.shape[1:]
    rows = height // (CHIPS * CORE)

    def halves(value):
        return (
            lax.dynamic_slice_in_dim(value, HALF * core, HALF, 0),
            lax.dynamic_slice_in_dim(value, HALF * (1 - core), HALF, 0),
        )

    def join_rows(keep, came):
        return jnp.where(
            core == 0,
            jnp.concatenate([keep, came], axis=1),
            jnp.concatenate([came, keep], axis=1),
        )

    def to_chip_rows(value):
        keep, give = halves(value)
        return join_rows(keep, core_swap(give))

    def join_slots(keep, came):
        return jnp.where(
            core == 0,
            jnp.concatenate([keep, came], axis=0),
            jnp.concatenate([came, keep], axis=0),
        )

    parts = pltpu.with_memory_space_constraint(
        grads[0].reshape(blocks, CHIPS, CORE, rows, width), pltpu.HBM
    )
    at_dp = lax.axis_index(("y", "zl", "core")).astype(jnp.int32)[None]
    r_near, r_late = z_swap(root_right[:HALF]), z_swap(root_right[HALF:])
    chip = pair_call(half_call(at_dp, parts, False), core_swap(half_call(at_dp, parts, True)))
    chip, r_near = lax.optimization_barrier((chip, r_near))
    r_near = jnp.concatenate([r_near, r_late], axis=0)
    r_keep, r_give = halves(
        jnp.where(
            zl == 0, jnp.stack([root_right, r_near], axis=1), jnp.stack([r_near, root_right], axis=1)
        )
    )
    r_came = core_swap(r_give)
    pair = jnp.where(
        core == 0, jnp.stack([r_keep, r_came], axis=2), jnp.stack([r_came, r_keep], axis=2)
    ).reshape(HALF, ZL * CORE * rows, width)
    parts = lax.all_to_all(chip, ("y", "zl"), 0, 0, tiled=True)

    slot = slot_index(owner, CAP)
    owners = X * ZH
    me = x * ZH + zh
    mine_of = lax.dynamic_slice_in_dim(owner, me * BPD, BPD, 0)
    hit = mine_of[None, :] == jnp.arange(owners, dtype=jnp.int32)[:, None]
    order = jnp.arange(BPD, dtype=jnp.int32)
    to = BPD + jnp.maximum(jnp.sum(jnp.where(hit, order[None, :] - BPD, 0), axis=1), -BPD)
    target = me * CAP + jnp.arange(CAP, dtype=jnp.int32)
    source = jnp.arange(owners * BPD, dtype=jnp.int32) // BPD + 1
    held = jnp.sum(jnp.where(slot[None, :] == target[:, None], source[None, :], 0), axis=1) - 1

    left2 = to_chip_rows(root_left)
    weights2 = to_chip_rows(weights)
    left2, weights2, to, held, parts = lax.optimization_barrier(
        (left2, weights2, to, held, parts)
    )
    sends, pair = lax.optimization_barrier((sort_call(to, parts), pair))
    came = lax.all_to_all(sends, ("x", "zh"), 0, 0, tiled=True)
    r_all = (pair, y_up(pair), y_down(pair), y_two(pair))
    mine = pick_call(held, came)
    mine, r_all = lax.optimization_barrier((mine, r_all))

    g_all = gather_chips(to_chip_rows(mine))

    mine, _ = lax.optimization_barrier((mine, g_all[1]))
    grad32 = mine.astype(F32)
    new_second = 0.9 * adam_second + 0.1 * grad32 * grad32
    adam_dir = grad32 / (jnp.sqrt(new_second) + 1e-08)
    adam_keep, adam_give = halves(jnp.sum(adam_dir * adam_dir, axis=(1, 2)))
    adam_sq = adam_keep + core_swap(adam_give)

    precond, sums, g_full = precond_call(at_dp, adam_sq, left2, g_all, r_all)
    sums = lax.all_to_all(sums, ("y", "zl"), 0, 0, tiled=True)
    prods = stats_call(at_dp, g_full, rows)
    lkeep, lgive, rkeep, rgive = prods
    sums, lcame, rcame = lax.optimization_barrier((sums, core_swap(lgive), core_swap(rgive)))
    precond = pltpu.with_memory_space_constraint(precond, pltpu.HBM)
    fresh = fresh_call(sums, weights2, precond)

    n_all = gather_chips(fresh)
    n_all[:5] = lax.optimization_barrier(n_all[:5])
    new_left = 0.5 * stat_left + 0.5 * join_slots(lkeep, lcame)
    new_right = 0.5 * stat_right + 0.5 * join_slots(rkeep, rcame)
    n_all[7], new_left, new_right = lax.optimization_barrier((n_all[7], new_left, new_right))
    n_other = [core_swap(p) for p in n_all]
    new_weights = assemble_call(at_dp, n_all, n_other)
    return (new_weights, new_left, new_right, new_second)


def solution(mesh):
    fine = Mesh(mesh.devices.reshape(Y, ZL, CORE, X, ZH), ("y", "zl", "core", "x", "zh"))
    dp, own = ("y", "zl", "core"), ("x", "zh")
    rows = P(own, dp, None)
    return jax.shard_map(
        on_device,
        mesh=fine,
        in_specs=(P(dp, own, None, None), P()) + (rows,) * 6,
        out_specs=(P(own, None, None), rows, rows, rows),
        check_vma=False,
    )
```
